256 devices in a mesh: dp: 64 (over z, y, core), group: 4 (over x).
Axes of the slice: x: 4, y: 4, z: 8, core: 2. Of those that a mesh axis runs over, the one named last changes fastest.
Arguments:
- frames: bfloat16 [4, 36864, 2048], P('group', 'dp'), may hold values from -6 to 6
- lengths: int32 [4, 192], P('group', 'dp'), may hold values from 24 to 192, as said below
- destination: int32 [4, 192], P('group', 'dp'), may hold values from 0 to 63, as said below
- offsets: int32 [4, 192], P('group', 'dp'), may hold values from 0 to 360, as said below
- norm_gain: bfloat16 [2048], P(('dp', 'group')), may hold values from 0.099609375 to 1.8984375
- weight_in: bfloat16 [2048, 4096], P(('dp', 'group')), may hold values from -0.125 to 0.125
- depth_kernel: bfloat16 [2048, 32], P(('dp', 'group')), may hold values from -1 to 1
- post_gain: bfloat16 [2048], P(('dp', 'group')), may hold values from 0.099609375 to 1.8984375
- weight_out: bfloat16 [2048, 2048], P(('dp', 'group')), may hold values from -0.125 to 0.125
Outputs:
- mixed: bfloat16 [4, 24576, 2048], P('group', 'dp')
The draws below stay inside these ranges and needn't reach their ends.
Inputs may be any that keep to these rules, and one draw needn't show every extreme that they name: `destination`: every device of a group sends exactly one utterance to itself, one to dp index + 1 and one to dp index - 1, both taken modulo 64, within its own group index. `lengths`: every device receives utterances with 384 frames in all; one utterance of each device's receipts has exactly 192 frames; in every group some device's slots are full. `offsets`: the utterances that one device receives lie back to back without gaps or intersection over its 384 rows.
All inputs are finite; a program needn't handle non-finite values.
Results may differ from the reference program's by a relative error of at most 0.0085.
Values may be sent and summed in bfloat16 or wider, within the bound.
A program may use at most 128 MiB of HBM per device.

```python
import jax
import jax.numpy as jnp
from jax import lax

D = 2048
KERNEL = 32
MAXLEN = 192
UTT_DEV = 3
LMIN = 24
RCV_DEV = 384
FR_DEV = 576
RCV_ALL = 24576
FR_ALL = 36864
UTT_ALL = 192
N_DP = 64
N_GROUP = 4


def layout(key):
    base = jax.random.fold_in(key, 17)
    key_full, key_split, key_long, key_order, key_slot = jax.random.split(base, 5)
    full_device = jax.random.randint(key_full, (N_GROUP, 1), 0, N_DP)
    first_len = jax.random.randint(key_split, (N_GROUP, N_DP), LMIN, MAXLEN - LMIN + 1)
    second_len = MAXLEN - first_len
    long_rel = jax.random.randint(key_long, (N_GROUP, N_DP), 0, 3)
    receiver = jnp.arange(N_DP, dtype=jnp.int32)[None, :]
    distance = (receiver - full_device) % N_DP
    forced = jnp.where(distance == 0, 1, jnp.where(distance == 1, 2, jnp.where(distance == N_DP - 1, 0, long_rel)))
    rel_index = jnp.arange(3, dtype=jnp.int32)[None, None, :]
    other_rank = (rel_index - forced[..., None]) % 3
    per_dest_len = jnp.where(other_rank == 0, MAXLEN, jnp.where(other_rank == 1, first_len[..., None], second_len[..., None]))
    rotate = jax.random.randint(key_order, (N_GROUP, N_DP, 1), 0, 3)
    placed = (rel_index + rotate) % 3
    earlier = (placed[..., None, :] < placed[..., :, None]).astype(jnp.int32)
    per_dest_off = jnp.sum(per_dest_len[..., None, :] * earlier, axis=-1)
    src_len = jnp.stack([jnp.roll(per_dest_len[:, :, index], -(index - 1), axis=1) for index in range(3)], axis=2)
    src_off = jnp.stack([jnp.roll(per_dest_off[:, :, index], -(index - 1), axis=1) for index in range(3)], axis=2)
    sources = jnp.arange(N_DP, dtype=jnp.int32)[None, :, None]
    src_dest = jnp.broadcast_to((sources + rel_index - 1) % N_DP, (N_GROUP, N_DP, 3))
    slot_turn = jax.random.randint(key_slot, (N_GROUP, N_DP, 1), 0, 3)
    order = (jnp.arange(3, dtype=jnp.int32)[None, None, :] + slot_turn) % 3
    lengths_out = jnp.take_along_axis(src_len, order, axis=2).reshape(N_GROUP, N_DP * 3)
    dest_out = jnp.take_along_axis(src_dest, order, axis=2).reshape(N_GROUP, N_DP * 3)
    offsets_out = jnp.take_along_axis(src_off, order, axis=2).reshape(N_GROUP, N_DP * 3)
    return (lengths_out.astype(jnp.int32), dest_out.astype(jnp.int32), offsets_out.astype(jnp.int32))


def draw_lengths(key, part):
    return layout(key)[0]


def draw_destination(key, part):
    return layout(key)[1]


def draw_offsets(key, part):
    return layout(key)[2]


def block_scale(rng, dims, shards, least, top_value):
    def one(dim, shards_of):
        heights = jax.random.uniform(jax.random.fold_in(jax.random.fold_in(rng, 6), dim), (shards_of,), jnp.float32, least / len(shards), top_value / len(shards))
        return jnp.repeat(jnp.exp(heights), dims[dim] // shards_of).reshape((-1,) + (1,) * (len(dims) - dim - 1))

    gain = one(*shards[0])
    for cut in shards[1:]:
        gain = gain * one(*cut)
    return gain


def noise(key, shape, scale, limit, cuts=(), held_as=jnp.bfloat16):
    entries = jax.random.normal(key, shape, jnp.float32) * scale
    if len(cuts) > 0:
        entries = block_scale(key, shape, cuts, -0.22, 0.18) * entries
    return jnp.clip(entries, min=-limit, max=limit).astype(held_as)


def setup_inputs(seed: int = 0) -> dict:
    keys = jax.random.split(jax.random.key(seed), 10)
    frames = noise(keys[0], (N_GROUP, FR_ALL, D), 1.0, 6.0, ((0, 4), (1, 64)))
    lengths = draw_lengths(jax.random.fold_in(keys[9], 71), 0)
    destination = draw_destination(jax.random.fold_in(keys[9], 71), 0)
    offsets = draw_offsets(jax.random.fold_in(keys[9], 71), 0)
    norm_gain = jnp.clip(1.0 + 0.18 * jax.random.normal(keys[4], (D,), jnp.float32), 0.099609375, 1.8984375).astype(jnp.bfloat16)
    weight_in = noise(keys[5], (D, 2 * D), D ** -0.5, 0.125, ((0, 256),))
    depth_kernel = noise(keys[6], (D, KERNEL), KERNEL ** -0.5, 1.0, ((0, 256),))
    post_gain = jnp.clip(1.0 + 0.18 * jax.random.normal(keys[7], (D,), jnp.float32), 0.099609375, 1.8984375).astype(jnp.bfloat16)
    weight_out = noise(keys[8], (D, D), D ** -0.5, 0.125, ((0, 256),))
    return {"frames": frames, "lengths": lengths, "destination": destination, "offsets": offsets, "norm_gain": norm_gain, "weight_in": weight_in, "depth_kernel": depth_kernel, "post_gain": post_gain, "weight_out": weight_out}


epsilon = 1e-05

def layer_norm(values, scale_gain):
    center = values - lax.optimization_barrier(jnp.mean(values, axis=-1, keepdims=True))
    spread = lax.optimization_barrier(jnp.mean(center * center, axis=-1, keepdims=True))
    return center * lax.rsqrt(spread + epsilon) * scale_gain.astype(jnp.float32)

def conv_module(inputs, segment, norm_gain, weight_in, depth_kernel, post_gain, weight_out):
    row_count = inputs.shape[0]
    widths = inputs.shape[1]
    source = inputs.astype(jnp.float32)
    normed = layer_norm(source, norm_gain).astype(jnp.bfloat16)
    projected = jnp.dot(normed, weight_in, preferred_element_type=jnp.float32)
    gated_rows = projected[:, :widths] * jax.nn.sigmoid(projected[:, widths:])
    margin = KERNEL // 2
    padded = jnp.pad(gated_rows, ((margin, margin), (0, 0)))
    labels = jnp.pad(segment, (margin, margin), constant_values=-1)
    kernel_rows = depth_kernel.astype(jnp.float32)
    depthwise = jnp.zeros_like(gated_rows)
    for column in range(KERNEL):
        inside = (labels[column:column + row_count] == segment)[:, None]
        depthwise = depthwise + jnp.where(inside, padded[column:column + row_count], 0.0) * kernel_rows[:, column]
    normed_post = layer_norm(depthwise, post_gain)
    active = (normed_post * jax.nn.sigmoid(normed_post)).astype(jnp.bfloat16)
    return (source + jnp.dot(active, weight_out, preferred_element_type=jnp.float32)).astype(jnp.bfloat16)

def rebalance_map(lengths, destination, offsets):
    lengths = lengths.astype(jnp.int32)
    destination = destination.astype(jnp.int32)
    offsets = offsets.astype(jnp.int32)
    per_source = lengths.reshape(-1, UTT_DEV)
    starts = (jnp.cumsum(per_source, axis=1).astype(jnp.int32) - per_source).reshape(-1)
    sender = jnp.arange(UTT_ALL, dtype=jnp.int32) // UTT_DEV
    frame_step = jnp.arange(MAXLEN, dtype=jnp.int32)
    valid_rows = frame_step[None, :] < lengths[:, None]
    target = jnp.where(valid_rows, destination[:, None] * RCV_DEV + offsets[:, None] + frame_step[None, :], RCV_ALL)
    anchor = sender[:, None] * FR_DEV + starts[:, None] + frame_step[None, :]
    names = jnp.broadcast_to(jnp.arange(UTT_ALL, dtype=jnp.int32)[:, None] + 1, target.shape)
    pick_rows = jnp.zeros((RCV_ALL,), jnp.int32).at[target.reshape(-1)].set(anchor.reshape(-1).astype(jnp.int32), mode='drop')
    labels = jnp.zeros((RCV_ALL,), jnp.int32).at[target.reshape(-1)].set(names.reshape(-1), mode='drop')
    return (pick_rows, labels)

def reference(frames, lengths, destination, offsets, norm_gain, weight_in, depth_kernel, post_gain, weight_out):

    def one_group(items):
        group_frames, group_lengths, group_dest, group_offsets = items
        pick_rows, labels = rebalance_map(group_lengths, group_dest, group_offsets)
        balanced = group_frames[pick_rows]
        return conv_module(balanced, labels, norm_gain, weight_in, depth_kernel, post_gain, weight_out)
    return lax.map(one_group, (frames, lengths, destination, offsets))
```

```python
import jax
import jax.numpy as jnp
from jax import lax
from jax.sharding import PartitionSpec as P

D = 2048
KERNEL = 32
MAXLEN = 192
RCV_DEV = 384
IN_CHUNKS = 4
OUT_CHUNKS = 2


epsilon = 1e-05


def shifted(array, axis, by):
    peers = lax.axis_size(axis)
    return lax.ppermute(array, axis, [(i, (i + by) % peers) for i in range(peers)])


def layer_norm(values, scale_gain):
    center = values - jnp.mean(values, axis=-1, keepdims=True)
    spread = jnp.mean(center * center, axis=-1, keepdims=True)
    return center * lax.rsqrt(spread + epsilon) * scale_gain.astype(jnp.float32)


def depth_pass(gated_rows, segment, kernel_rows):
    row_count = gated_rows.shape[0]
    margin = KERNEL // 2
    padded = jnp.pad(gated_rows, ((margin, margin), (0, 0)))
    labels = jnp.pad(segment, (margin, margin), constant_values=-1)
    depthwise = jnp.zeros_like(gated_rows)
    for column in range(KERNEL):
        inside = (labels[column : column + row_count] == segment)[:, None]
        depthwise = (
            depthwise
            + jnp.where(inside, padded[column : column + row_count], 0.0) * kernel_rows[:, column]
        )
    return depthwise


def relocate(own_part, next_part, prev_part):
    from_prev = shifted((next_part[0], next_part[1]), "dp", 1)
    from_next = shifted((prev_part[0], prev_part[1]), "dp", -1)
    received = jnp.zeros((RCV_DEV + MAXLEN, D), jnp.bfloat16)
    segment = jnp.zeros((RCV_DEV,), jnp.int32)
    position = jnp.arange(RCV_DEV, dtype=jnp.int32)
    arrivals = (own_part, from_prev, from_next)
    for label_id in range(3):
        frame_rows, meta_data = arrivals[label_id]
        current = lax.dynamic_slice_in_dim(received, meta_data[1], MAXLEN, 0)
        received = lax.dynamic_update_slice_in_dim(received, current + frame_rows, meta_data[1], 0)
        inside = (position >= meta_data[1]) & (position < meta_data[1] + meta_data[0])
        segment = jnp.where(inside, label_id + 1, segment)
    return (received[:RCV_DEV], segment)


def shards(
    frames, lengths, destination, offsets, norm_gain, weight_in, depth_kernel, post_gain, weight_out
):
    axes = ("dp", "group")
    small = jnp.concatenate(
        [norm_gain.reshape(-1, 1), post_gain.reshape(-1, 1), depth_kernel], axis=1
    )
    width = D // IN_CHUNKS
    in_parts = []
    for c in range(IN_CHUNKS):
        columns = [
            weight_in[:, c * width : (c + 1) * width],
            weight_in[:, D + c * width : D + (c + 1) * width],
        ]
        if c == 0:
            columns.append(small)
        in_parts.append(lax.all_gather(jnp.concatenate(columns, axis=1), axes, axis=0, tiled=True))
    small_all = in_parts[0][:, 2 * width :]
    in_parts[0] = in_parts[0][:, : 2 * width]
    out_width = D // OUT_CHUNKS
    out_parts = [
        lax.all_gather(weight_out[:, m * out_width : (m + 1) * out_width], axes, axis=0, tiled=True)
        for m in range(OUT_CHUNKS)
    ]
    norm_full = small_all[:, 0]
    post_full = small_all[:, 1]
    kernel_full = small_all[:, 2:].astype(jnp.float32)

    dp_count = lax.axis_size("dp")
    my_index = lax.axis_index("dp")
    local_frames = frames[0]
    lengths_here = lengths[0]
    dest_here = destination[0]
    offsets_here = offsets[0]
    starts = jnp.cumsum(lengths_here) - lengths_here
    relative = (dest_here - my_index) % dp_count
    slot_ids = jnp.arange(3, dtype=jnp.int32)

    def pick_entry(values, which):
        return jnp.sum(jnp.where(slot_ids == which, values, 0))

    def slot_of(code):
        return jnp.sum(jnp.where(relative == code, slot_ids, 0))

    chosen = (slot_of(0), slot_of(1), slot_of(dp_count - 1))

    def cut_utterance(source_rows, which):
        start_row = pick_entry(starts, which)
        live_count = pick_entry(lengths_here, which)
        frame_rows = lax.dynamic_slice_in_dim(source_rows, start_row, MAXLEN, 0)
        keep_rows = jnp.arange(MAXLEN, dtype=jnp.int32) < live_count
        kept = jnp.where(keep_rows[:, None], frame_rows, jnp.zeros_like(frame_rows))
        return (kept, jnp.stack([live_count, pick_entry(offsets_here, which)]))

    received, segment = relocate(
        cut_utterance(local_frames, chosen[0]),
        cut_utterance(local_frames, chosen[1]),
        cut_utterance(local_frames, chosen[2]),
    )
    source = received.astype(jnp.float32)
    normed = layer_norm(source, norm_full).astype(jnp.bfloat16)
    pieces = []
    for c in range(IN_CHUNKS):
        projected = jnp.dot(normed, in_parts[c], preferred_element_type=jnp.float32)
        gated = projected[:, :width] * jax.nn.sigmoid(projected[:, width:])
        pieces.append(depth_pass(gated, segment, kernel_full[c * width : (c + 1) * width]))
    depthwise = jnp.concatenate(pieces, axis=1)
    normed_post = layer_norm(depthwise, post_full)
    active = (normed_post * jax.nn.sigmoid(normed_post)).astype(jnp.bfloat16)
    outs = []
    for m in range(OUT_CHUNKS):
        mixed = source[:, m * out_width : (m + 1) * out_width] + jnp.dot(
            active, out_parts[m], preferred_element_type=jnp.float32
        )
        outs.append(mixed.astype(jnp.bfloat16))
    return jnp.concatenate(outs, axis=1)[None]


def solution(mesh):
    placed = (
        P("group", "dp", None),
        P("group", "dp"),
        P("group", "dp"),
        P("group", "dp"),
        P(("dp", "group")),
        P(("dp", "group"), None),
        P(("dp", "group"), None),
        P(("dp", "group")),
        P(("dp", "group"), None),
    )
    return jax.shard_map(
        shards, mesh=mesh, in_specs=placed, out_specs=P("group", "dp", None), check_vma=False
    )
```

```python
import jax
import jax.numpy as jnp
from jax import lax
from jax.experimental import pallas as pl
from jax.experimental.pallas import tpu as pltpu
from jax.sharding import PartitionSpec as P

D = 2048
KERNEL = 32
MAXLEN = 192
RCV_DEV = 384


epsilon = 1e-05


def shifted(array, axis, by):
    peers = lax.axis_size(axis)
    return lax.ppermute(array, axis, [(i, (i + by) % peers) for i in range(peers)])


def sent_together(arrays, axis, dim, along):
    columns = [a.reshape(*a.shape[:along], -1) for a in arrays]
    both = jnp.concatenate(columns, axis=along)
    out, at, done = (lax.all_gather(both, axis, axis=dim, tiled=True), 0, [])
    for a, column in zip(arrays, columns):
        slab = out[..., at : at + column.shape[along]]
        done.append(slab.reshape(*slab.shape[:along], *a.shape[along:]))
        at += column.shape[along]
    return tuple(done)


def layer_norm(values, scale_gain):
    center = values - jnp.mean(values, axis=-1, keepdims=True)
    spread = jnp.mean(center * center, axis=-1, keepdims=True)
    return center * lax.rsqrt(spread + epsilon) * scale_gain.astype(jnp.float32)


ROW_CHUNK = 128
LANE_BLOCK = 128


def depth_kernel_body(padded_ref, labels_ref, taps_ref, gain_ref, out_ref, mask_ref, acc_ref):
    rows = out_ref.shape[0]
    margin = KERNEL // 2
    for column in range(KERNEL):
        same = labels_ref[column : column + rows, :] == labels_ref[margin : margin + rows, :]
        mask_ref[column] = jnp.where(same, 1.0, 0.0)

    def lane_block(index, carry):
        lanes = pl.ds(pl.multiple_of(index * LANE_BLOCK, LANE_BLOCK), LANE_BLOCK)
        for chunk in range(rows // ROW_CHUNK):
            low = chunk * ROW_CHUNK
            total = jnp.zeros((ROW_CHUNK, LANE_BLOCK), jnp.float32)
            for column in range(KERNEL):
                shifted = padded_ref[low + column : low + column + ROW_CHUNK, lanes]
                weight = mask_ref[column, low : low + ROW_CHUNK, :]
                total = total + shifted * weight * taps_ref[column : column + 1, lanes]
            acc_ref[low : low + ROW_CHUNK, lanes] = total
        return carry

    lax.fori_loop(0, out_ref.shape[1] // LANE_BLOCK, lane_block, 0)
    for chunk in range(rows // ROW_CHUNK):
        low = chunk * ROW_CHUNK
        values = acc_ref[low : low + ROW_CHUNK, :]
        center = values - jnp.mean(values, axis=-1, keepdims=True)
        spread = jnp.mean(center * center, axis=-1, keepdims=True)
        normed = center * lax.rsqrt(spread + epsilon) * gain_ref[...]
        out_ref[low : low + ROW_CHUNK, :] = (normed * jax.nn.sigmoid(normed)).astype(out_ref.dtype)


def depth_and_norm(gated_rows, segment, taps, post_gain):
    rows, width = gated_rows.shape
    margin = KERNEL // 2
    padded = jnp.pad(gated_rows, ((margin, margin), (0, 0)))
    labels = jnp.pad(segment, (margin, margin), constant_values=-1)
    labels = jnp.broadcast_to(labels[:, None], (rows + 2 * margin, LANE_BLOCK))
    return pl.pallas_call(
        depth_kernel_body,
        out_shape=jax.ShapeDtypeStruct((rows, width), jnp.bfloat16),
        in_specs=[pl.BlockSpec(memory_space=pltpu.VMEM)] * 4,
        out_specs=pl.BlockSpec(memory_space=pltpu.VMEM),
        scratch_shapes=[
            pltpu.VMEM((KERNEL, rows, LANE_BLOCK), jnp.float32),
            pltpu.VMEM((rows, width), jnp.float32),
        ],
        compiler_params=pltpu.CompilerParams(vmem_limit_bytes=48 * 1024 * 1024),
        cost_estimate=pl.CostEstimate(
            flops=3 * KERNEL * rows * width, transcendentals=rows * width, bytes_accessed=6 * rows * width
        ),
    )(padded, labels, taps, post_gain)


def conv_module(inputs, segment, params):
    norm_gain, weight_in, taps, post_gain, weight_out = params
    widths = inputs.shape[1]
    source = inputs.astype(jnp.float32)
    normed = layer_norm(source, norm_gain).astype(jnp.bfloat16)
    projected = jnp.dot(normed, weight_in, preferred_element_type=jnp.float32)
    gated_rows = projected[:, :widths] * jax.nn.sigmoid(projected[:, widths:])
    active = depth_and_norm(gated_rows, segment, taps, post_gain)
    return (source + jnp.dot(active, weight_out, preferred_element_type=jnp.float32)).astype(
        jnp.bfloat16
    )


def relocate(own_part, next_part, prev_part):
    from_prev = shifted((next_part[0], next_part[1]), "dp", 1)
    from_next = shifted((prev_part[0], prev_part[1]), "dp", -1)
    received = jnp.zeros((RCV_DEV + MAXLEN, D), jnp.bfloat16)
    segment = jnp.zeros((RCV_DEV,), jnp.int32)
    position = jnp.arange(RCV_DEV, dtype=jnp.int32)
    arrivals = (own_part, from_prev, from_next)
    for label_id in range(3):
        frame_rows, meta_data = arrivals[label_id]
        current = lax.dynamic_slice_in_dim(received, meta_data[1], MAXLEN, 0)
        received = lax.dynamic_update_slice_in_dim(received, current + frame_rows, meta_data[1], 0)
        inside = (position >= meta_data[1]) & (position < meta_data[1] + meta_data[0])
        segment = jnp.where(inside, label_id + 1, segment)
    return (received[:RCV_DEV], segment)


def shards(
    frames, lengths, destination, offsets, norm_gain, weight_in, depth_kernel, post_gain, weight_out
):
    dp_count = lax.axis_size("dp")
    small = jnp.concatenate([norm_gain[:, None], post_gain[:, None], depth_kernel], axis=1)
    both = jnp.concatenate([weight_in, weight_out, small], axis=1)
    gathered = lax.all_gather(both, ("dp", "group"), axis=0, tiled=True)
    columns = weight_in.shape[1] + weight_out.shape[1]
    small_t = jnp.transpose(gathered[:, columns:]).astype(jnp.float32)
    params = (
        small_t[0:1],
        gathered[:, : weight_in.shape[1]],
        small_t[2:],
        small_t[1:2],
        gathered[:, weight_in.shape[1] : columns],
    )
    my_index = lax.axis_index("dp")
    local_frames = frames[0]
    lengths_here = lengths[0]
    dest_here = destination[0]
    offsets_here = offsets[0]
    starts = jnp.cumsum(lengths_here) - lengths_here
    relative = (dest_here - my_index) % dp_count
    slot_ids = jnp.arange(3, dtype=jnp.int32)

    def pick_entry(values, which):
        return jnp.sum(jnp.where(slot_ids == which, values, 0))

    def slot_of(code):
        return jnp.sum(jnp.where(relative == code, slot_ids, 0))

    chosen = (slot_of(0), slot_of(1), slot_of(dp_count - 1))

    def cut_utterance(source_rows, which):
        start_row = pick_entry(starts, which)
        live_count = pick_entry(lengths_here, which)
        frame_rows = lax.dynamic_slice_in_dim(source_rows, start_row, MAXLEN, 0)
        keep_rows = jnp.arange(MAXLEN, dtype=jnp.int32) < live_count
        kept = jnp.where(keep_rows[:, None], frame_rows, jnp.zeros_like(frame_rows))
        return (kept, jnp.stack([live_count, pick_entry(offsets_here, which)]))

    received, segment = relocate(
        cut_utterance(local_frames, chosen[0]),
        cut_utterance(local_frames, chosen[1]),
        cut_utterance(local_frames, chosen[2]),
    )
    mixed = conv_module(received, segment, params)
    return mixed[None]


def solution(mesh):
    placed = (
        P("group", "dp", None),
        P("group", "dp"),
        P("group", "dp"),
        P("group", "dp"),
        P(("dp", "group")),
        P(("dp", "group"), None),
        P(("dp", "group"), None),
        P(("dp", "group")),
        P(("dp", "group"), None),
    )
    return jax.shard_map(
        shards, mesh=mesh, in_specs=placed, out_specs=P("group", "dp", None), check_vma=False
    )
```

```python
import jax
import jax.numpy as jnp
from jax import lax
from jax.experimental import pallas as pl
from jax.experimental.pallas import tpu as pltpu
from jax.sharding import PartitionSpec as P

D = 2048
KERNEL = 32
MAXLEN = 192
RCV_DEV = 384


epsilon = 1e-05


def shifted(array, axis, by):
    peers = lax.axis_size(axis)
    return lax.ppermute(array, axis, [(i, (i + by) % peers) for i in range(peers)])


def sent_together(arrays, axis, dim, along):
    columns = [a.reshape(*a.shape[:along], -1) for a in arrays]
    both = jnp.concatenate(columns, axis=along)
    out, at, done = (lax.all_gather(both, axis, axis=dim, tiled=True), 0, [])
    for a, column in zip(arrays, columns):
        slab = out[..., at : at + column.shape[along]]
        done.append(slab.reshape(*slab.shape[:along], *a.shape[along:]))
        at += column.shape[along]
    return tuple(done)


def layer_norm(values, scale_gain):
    center = values - jnp.mean(values, axis=-1, keepdims=True)
    spread = jnp.mean(center * center, axis=-1, keepdims=True)
    return center * lax.rsqrt(spread + epsilon) * scale_gain.astype(jnp.float32)


ROW_CHUNK = 128
LANE_BLOCK = 128
BLOCK = 256


def fused_body(normed_ref, value_ref, gate_ref, labels_ref, taps_ref, gain_ref, out_ref, gated_ref, mask_ref, acc_ref):
    step = pl.program_id(0)
    blocks = pl.num_programs(0) - 1
    rows = out_ref.shape[0]
    margin = KERNEL // 2

    @pl.when(step == 0)
    def _():
        for column in range(KERNEL):
            same = labels_ref[column : column + rows, :] == labels_ref[margin : margin + rows, :]
            mask_ref[column] = jnp.where(same, 1.0, 0.0)
        gated_ref[...] = jnp.zeros(gated_ref.shape, jnp.float32)

    normed = normed_ref[...]
    projected = jnp.dot(normed, value_ref[...], preferred_element_type=jnp.float32)
    gates = jnp.dot(normed, gate_ref[...], preferred_element_type=jnp.float32)
    gated_ref[step % 2, margin : margin + rows, :] = projected * jax.nn.sigmoid(gates)

    done = jnp.maximum(step - 1, 0)
    slot = (step + 1) % 2
    for half in range(BLOCK // LANE_BLOCK):
        lanes = pl.ds(pl.multiple_of(done * BLOCK + half * LANE_BLOCK, LANE_BLOCK), LANE_BLOCK)
        inner = slice(half * LANE_BLOCK, (half + 1) * LANE_BLOCK)
        for chunk in range(rows // ROW_CHUNK):
            low = chunk * ROW_CHUNK
            total = jnp.zeros((ROW_CHUNK, LANE_BLOCK), jnp.float32)
            for column in range(KERNEL):
                shifted = gated_ref[slot, low + column : low + column + ROW_CHUNK, inner]
                weight = mask_ref[column, low : low + ROW_CHUNK, :]
                total = total + shifted * weight * taps_ref[column : column + 1, lanes]
            acc_ref[low : low + ROW_CHUNK, lanes] = total

    @pl.when(step == blocks)
    def _():
        for chunk in range(rows // ROW_CHUNK):
            low = chunk * ROW_CHUNK
            values = acc_ref[low : low + ROW_CHUNK, :]
            center = values - jnp.mean(values, axis=-1, keepdims=True)
            spread = jnp.mean(center * center, axis=-1, keepdims=True)
            normed_post = center * lax.rsqrt(spread + epsilon) * gain_ref[...]
            out_ref[low : low + ROW_CHUNK, :] = (
                normed_post * jax.nn.sigmoid(normed_post)
            ).astype(out_ref.dtype)


def fused_projection(normed, gathered, segment, taps, post_gain):
    rows, width = normed.shape
    margin = KERNEL // 2
    blocks = width // BLOCK
    labels = jnp.pad(segment, (margin, margin), constant_values=-1)
    labels = jnp.broadcast_to(labels[:, None], (rows + 2 * margin, LANE_BLOCK))
    last = blocks - 1
    whole = lambda s: (0, 0)
    return pl.pallas_call(
        fused_body,
        grid=(blocks + 1,),
        out_shape=jax.ShapeDtypeStruct((rows, width), jnp.bfloat16),
        in_specs=[
            pl.BlockSpec((rows, width), whole),
            pl.BlockSpec((width, BLOCK), lambda s: (0, jnp.minimum(s, last))),
            pl.BlockSpec((width, BLOCK), lambda s: (0, blocks + jnp.minimum(s, last))),
            pl.BlockSpec((rows + 2 * margin, LANE_BLOCK), whole),
            pl.BlockSpec((KERNEL, width), whole),
            pl.BlockSpec((1, width), whole),
        ],
        out_specs=pl.BlockSpec((rows, width), whole),
        scratch_shapes=[
            pltpu.VMEM((2, rows + 2 * margin, BLOCK), jnp.float32),
            pltpu.VMEM((KERNEL, rows, LANE_BLOCK), jnp.float32),
            pltpu.VMEM((rows, width), jnp.float32),
        ],
        compiler_params=pltpu.CompilerParams(
            dimension_semantics=("arbitrary",), vmem_limit_bytes=56 * 1024 * 1024
        ),
        cost_estimate=pl.CostEstimate(
            flops=2 * rows * width * 2 * width + 3 * KERNEL * rows * width,
            transcendentals=2 * rows * width,
            bytes_accessed=2 * width * 2 * width + 8 * rows * width,
        ),
    )(normed, gathered, gathered, labels, taps, post_gain)


def conv_module(inputs, segment, params):
    norm_gain, gathered, taps, post_gain, weight_out = params
    source = inputs.astype(jnp.float32)
    normed = layer_norm(source, norm_gain).astype(jnp.bfloat16)
    active = fused_projection(normed, gathered, segment, taps, post_gain)
    return (source + jnp.dot(active, weight_out, preferred_element_type=jnp.float32)).astype(
        jnp.bfloat16
    )


def relocate(own_part, next_part, prev_part):
    from_prev = shifted((next_part[0], next_part[1]), "dp", 1)
    from_next = shifted((prev_part[0], prev_part[1]), "dp", -1)
    received = jnp.zeros((RCV_DEV + MAXLEN, D), jnp.bfloat16)
    segment = jnp.zeros((RCV_DEV,), jnp.int32)
    position = jnp.arange(RCV_DEV, dtype=jnp.int32)
    arrivals = (own_part, from_prev, from_next)
    for label_id in range(3):
        frame_rows, meta_data = arrivals[label_id]
        current = lax.dynamic_slice_in_dim(received, meta_data[1], MAXLEN, 0)
        received = lax.dynamic_update_slice_in_dim(received, current + frame_rows, meta_data[1], 0)
        inside = (position >= meta_data[1]) & (position < meta_data[1] + meta_data[0])
        segment = jnp.where(inside, label_id + 1, segment)
    return (received[:RCV_DEV], segment)


def shards(
    frames, lengths, destination, offsets, norm_gain, weight_in, depth_kernel, post_gain, weight_out
):
    dp_count = lax.axis_size("dp")
    small = jnp.concatenate([norm_gain[:, None], post_gain[:, None], depth_kernel], axis=1)
    both = jnp.concatenate([weight_in, weight_out, small], axis=1)
    gathered = lax.all_gather(both, ("dp", "group"), axis=0, tiled=True)
    columns = weight_in.shape[1] + weight_out.shape[1]
    small_t = jnp.transpose(gathered[:, columns:]).astype(jnp.float32)
    params = (
        small_t[0:1],
        gathered,
        small_t[2:],
        small_t[1:2],
        gathered[:, weight_in.shape[1] : columns],
    )
    my_index = lax.axis_index("dp")
    local_frames = frames[0]
    lengths_here = lengths[0]
    dest_here = destination[0]
    offsets_here = offsets[0]
    starts = jnp.cumsum(lengths_here) - lengths_here
    relative = (dest_here - my_index) % dp_count
    slot_ids = jnp.arange(3, dtype=jnp.int32)

    def pick_entry(values, which):
        return jnp.sum(jnp.where(slot_ids == which, values, 0))

    def slot_of(code):
        return jnp.sum(jnp.where(relative == code, slot_ids, 0))

    chosen = (slot_of(0), slot_of(1), slot_of(dp_count - 1))

    def cut_utterance(source_rows, which):
        start_row = pick_entry(starts, which)
        live_count = pick_entry(lengths_here, which)
        frame_rows = lax.dynamic_slice_in_dim(source_rows, start_row, MAXLEN, 0)
        keep_rows = jnp.arange(MAXLEN, dtype=jnp.int32) < live_count
        kept = jnp.where(keep_rows[:, None], frame_rows, jnp.zeros_like(frame_rows))
        return (kept, jnp.stack([live_count, pick_entry(offsets_here, which)]))

    received, segment = relocate(
        cut_utterance(local_frames, chosen[0]),
        cut_utterance(local_frames, chosen[1]),
        cut_utterance(local_frames, chosen[2]),
    )
    mixed = conv_module(received, segment, params)
    return mixed[None]


def solution(mesh):
    placed = (
        P("group", "dp", None),
        P("group", "dp"),
        P("group", "dp"),
        P("group", "dp"),
        P(("dp", "group")),
        P(("dp", "group"), None),
        P(("dp", "group"), None),
        P(("dp", "group")),
        P(("dp", "group"), None),
    )
    return jax.shard_map(
        shards, mesh=mesh, in_specs=placed, out_specs=P("group", "dp", None), check_vma=False
    )
```

```python
import jax
import jax.numpy as jnp
from jax import lax
from jax.experimental import pallas as pl
from jax.experimental.pallas import tpu as pltpu
from jax.sharding import PartitionSpec as P

D = 2048
KERNEL = 32
MAXLEN = 192
RCV_DEV = 384


epsilon = 1e-05


def shifted(array, axis, by):
    peers = lax.axis_size(axis)
    return lax.ppermute(array, axis, [(i, (i + by) % peers) for i in range(peers)])


def sent_together(arrays, axis, dim, along):
    columns = [a.reshape(*a.shape[:along], -1) for a in arrays]
    both = jnp.concatenate(columns, axis=along)
    out, at, done = (lax.all_gather(both, axis, axis=dim, tiled=True), 0, [])
    for a, column in zip(arrays, columns):
        slab = out[..., at : at + column.shape[along]]
        done.append(slab.reshape(*slab.shape[:along], *a.shape[along:]))
        at += column.shape[along]
    return tuple(done)


def layer_norm(values, scale_gain):
    center = values - jnp.mean(values, axis=-1, keepdims=True)
    spread = jnp.mean(center * center, axis=-1, keepdims=True)
    return center * lax.rsqrt(spread + epsilon) * scale_gain.astype(jnp.float32)


SMALL_WIDTH = 128


def depth_pass(gated_rows, segment, taps):
    row_count = gated_rows.shape[0]
    margin = KERNEL // 2
    padded = jnp.pad(gated_rows, ((margin, margin), (0, 0)))
    labels = jnp.pad(segment, (margin, margin), constant_values=-1)
    depthwise = jnp.zeros_like(gated_rows)
    for column in range(KERNEL):
        inside = (labels[column : column + row_count] == segment)[:, None]
        depthwise = depthwise + jnp.where(inside, padded[column : column + row_count], 0.0) * taps[column : column + 1]
    return depthwise


def transpose_body(small_ref, out_ref):
    out_ref[...] = jnp.transpose(small_ref[...].astype(jnp.float32))


def small_rows(small_columns):
    count, width = small_columns.shape
    return pl.pallas_call(
        transpose_body,
        out_shape=jax.ShapeDtypeStruct((width, count), jnp.float32),
        in_specs=[pl.BlockSpec(memory_space=pltpu.VMEM)],
        out_specs=pl.BlockSpec(memory_space=pltpu.VMEM),
    )(small_columns)


def conv_module(inputs, segment, params):
    norm_gain, weight_in, taps, post_gain, weight_out = params
    widths = inputs.shape[1]
    source = inputs.astype(jnp.float32)
    normed = layer_norm(source, norm_gain).astype(jnp.bfloat16)
    projected = jnp.dot(normed, weight_in, preferred_element_type=jnp.float32)
    gated_rows = projected[:, :widths] * jax.nn.sigmoid(projected[:, widths:])
    depthwise = depth_pass(gated_rows, segment, taps)
    normed_post = layer_norm(depthwise, post_gain)
    active = (normed_post * jax.nn.sigmoid(normed_post)).astype(jnp.bfloat16)
    return (source + jnp.dot(active, weight_out, preferred_element_type=jnp.float32)).astype(
        jnp.bfloat16
    )


def relocate(own_part, next_part, prev_part):
    from_prev = shifted((next_part[0], next_part[1]), "dp", 1)
    from_next = shifted((prev_part[0], prev_part[1]), "dp", -1)
    received = jnp.zeros((RCV_DEV + MAXLEN, D), jnp.bfloat16)
    segment = jnp.zeros((RCV_DEV,), jnp.int32)
    position = jnp.arange(RCV_DEV, dtype=jnp.int32)
    arrivals = (own_part, from_prev, from_next)
    for label_id in range(3):
        frame_rows, meta_data = arrivals[label_id]
        current = lax.dynamic_slice_in_dim(received, meta_data[1], MAXLEN, 0)
        received = lax.dynamic_update_slice_in_dim(received, current + frame_rows, meta_data[1], 0)
        inside = (position >= meta_data[1]) & (position < meta_data[1] + meta_data[0])
        segment = jnp.where(inside, label_id + 1, segment)
    return (received[:RCV_DEV], segment)


def shards(
    frames, lengths, destination, offsets, norm_gain, weight_in, depth_kernel, post_gain, weight_out
):
    dp_count = lax.axis_size("dp")
    small = jnp.concatenate([norm_gain[:, None], post_gain[:, None], depth_kernel], axis=1)
    small = jnp.pad(small, ((0, 0), (0, SMALL_WIDTH - small.shape[1])))
    both = jnp.concatenate([weight_in, weight_out, small], axis=1)
    gathered = lax.all_gather(both, ("dp", "group"), axis=0, tiled=True)
    columns = weight_in.shape[1] + weight_out.shape[1]
    small_t = small_rows(gathered[:, columns:])
    params = (
        small_t[0:1],
        gathered[:, : weight_in.shape[1]],
        small_t[2 : 2 + KERNEL],
        small_t[1:2],
        gathered[:, weight_in.shape[1] : columns],
    )
    my_index = lax.axis_index("dp")
    local_frames = frames[0]
    lengths_here = lengths[0]
    dest_here = destination[0]
    offsets_here = offsets[0]
    starts = jnp.cumsum(lengths_here) - lengths_here
    relative = (dest_here - my_index) % dp_count
    slot_ids = jnp.arange(3, dtype=jnp.int32)

    def pick_entry(values, which):
        return jnp.sum(jnp.where(slot_ids == which, values, 0))

    def slot_of(code):
        return jnp.sum(jnp.where(relative == code, slot_ids, 0))

    chosen = (slot_of(0), slot_of(1), slot_of(dp_count - 1))

    def cut_utterance(source_rows, which):
        start_row = pick_entry(starts, which)
        live_count = pick_entry(lengths_here, which)
        frame_rows = lax.dynamic_slice_in_dim(source_rows, start_row, MAXLEN, 0)
        keep_rows = jnp.arange(MAXLEN, dtype=jnp.int32) < live_count
        kept = jnp.where(keep_rows[:, None], frame_rows, jnp.zeros_like(frame_rows))
        return (kept, jnp.stack([live_count, pick_entry(offsets_here, which)]))

    received, segment = relocate(
        cut_utterance(local_frames, chosen[0]),
        cut_utterance(local_frames, chosen[1]),
        cut_utterance(local_frames, chosen[2]),
    )
    mixed = conv_module(received, segment, params)
    return mixed[None]


def solution(mesh):
    placed = (
        P("group", "dp", None),
        P("group", "dp"),
        P("group", "dp"),
        P("group", "dp"),
        P(("dp", "group")),
        P(("dp", "group"), None),
        P(("dp", "group"), None),
        P(("dp", "group")),
        P(("dp", "group"), None),
    )
    return jax.shard_map(
        shards, mesh=mesh, in_specs=placed, out_specs=P("group", "dp", None), check_vma=False
    )
```

```python
import jax
import jax.numpy as jnp
from jax import lax
from jax.experimental import pallas as pl
from jax.experimental.pallas import tpu as pltpu
from jax.sharding import PartitionSpec as P

D = 2048
KERNEL = 32
MAXLEN = 192
RCV_DEV = 384


epsilon = 1e-05


def shifted(array, axis, by):
    peers = lax.axis_size(axis)
    return lax.ppermute(array, axis, [(i, (i + by) % peers) for i in range(peers)])


def sent_together(arrays, axis, dim, along):
    columns = [a.reshape(*a.shape[:along], -1) for a in arrays]
    both = jnp.concatenate(columns, axis=along)
    out, at, done = (lax.all_gather(both, axis, axis=dim, tiled=True), 0, [])
    for a, column in zip(arrays, columns):
        slab = out[..., at : at + column.shape[along]]
        done.append(slab.reshape(*slab.shape[:along], *a.shape[along:]))
        at += column.shape[along]
    return tuple(done)


def layer_norm(values, scale_gain):
    center = values - jnp.mean(values, axis=-1, keepdims=True)
    spread = jnp.mean(center * center, axis=-1, keepdims=True)
    return center * lax.rsqrt(spread + epsilon) * scale_gain.astype(jnp.float32)


SMALL_WIDTH = 128


def depth_pass(gated_rows, segment, taps):
    row_count = gated_rows.shape[0]
    margin = KERNEL // 2
    padded = jnp.pad(gated_rows, ((margin, margin), (0, 0)))
    labels = jnp.pad(segment, (margin, margin), constant_values=-1)
    depthwise = jnp.zeros_like(gated_rows)
    for column in range(KERNEL):
        inside = (labels[column : column + row_count] == segment)[:, None]
        depthwise = depthwise + jnp.where(inside, padded[column : column + row_count], 0.0) * taps[column : column + 1]
    return depthwise


def transpose_body(small_ref, out_ref):
    out_ref[...] = jnp.transpose(small_ref[...].astype(jnp.float32))


def small_rows(small_columns):
    count, width = small_columns.shape
    return pl.pallas_call(
        transpose_body,
        out_shape=jax.ShapeDtypeStruct((width, count), jnp.float32),
        in_specs=[pl.BlockSpec(memory_space=pltpu.VMEM)],
        out_specs=pl.BlockSpec(memory_space=pltpu.VMEM),
    )(small_columns)


def conv_module(inputs, segment, params):
    norm_gain, weight_in, taps, post_gain, weight_out = params
    widths = inputs.shape[1]
    source = inputs.astype(jnp.float32)
    normed = layer_norm(source, norm_gain).astype(jnp.bfloat16)
    projected = jnp.dot(normed, weight_in, preferred_element_type=jnp.float32)
    gated_rows = projected[:, :widths] * jax.nn.sigmoid(projected[:, widths:])
    depthwise = depth_pass(gated_rows, segment, taps)
    normed_post = layer_norm(depthwise, post_gain)
    active = (normed_post * jax.nn.sigmoid(normed_post)).astype(jnp.bfloat16)
    return (source + jnp.dot(active, weight_out, preferred_element_type=jnp.float32)).astype(
        jnp.bfloat16
    )


def relocate(own_part, next_part, prev_part):
    from_prev = shifted((next_part[0], next_part[1]), "dp", 1)
    from_next = shifted((prev_part[0], prev_part[1]), "dp", -1)
    received = jnp.zeros((RCV_DEV + MAXLEN, D), jnp.bfloat16)
    segment = jnp.zeros((RCV_DEV,), jnp.int32)
    position = jnp.arange(RCV_DEV, dtype=jnp.int32)
    arrivals = (own_part, from_prev, from_next)
    for label_id in range(3):
        frame_rows, meta_data = arrivals[label_id]
        current = lax.dynamic_slice_in_dim(received, meta_data[1], MAXLEN, 0)
        received = lax.dynamic_update_slice_in_dim(received, current + frame_rows, meta_data[1], 0)
        inside = (position >= meta_data[1]) & (position < meta_data[1] + meta_data[0])
        segment = jnp.where(inside, label_id + 1, segment)
    return (received[:RCV_DEV], segment)


def shards(
    frames, lengths, destination, offsets, norm_gain, weight_in, depth_kernel, post_gain, weight_out
):
    dp_count = lax.axis_size("dp")
    small = jnp.concatenate([norm_gain[:, None], post_gain[:, None], depth_kernel], axis=1)
    small = jnp.pad(small, ((0, 0), (0, SMALL_WIDTH - small.shape[1])))
    both = jnp.concatenate([weight_in, weight_out], axis=1)
    gathered = lax.all_gather(both, ("dp", "group"), axis=0, tiled=True)
    columns = weight_in.shape[1] + weight_out.shape[1]
    peers = lax.axis_size(("dp", "group"))
    copies = jnp.broadcast_to(small[None], (peers,) + small.shape)
    spread = lax.all_to_all(copies, ("dp", "group"), 0, 0, tiled=True)
    small_t = small_rows(spread.reshape(-1, SMALL_WIDTH))
    params = (
        small_t[0:1],
        gathered[:, : weight_in.shape[1]],
        small_t[2 : 2 + KERNEL],
        small_t[1:2],
        gathered[:, weight_in.shape[1] : columns],
    )
    my_index = lax.axis_index("dp")
    local_frames = frames[0]
    lengths_here = lengths[0]
    dest_here = destination[0]
    offsets_here = offsets[0]
    starts = jnp.cumsum(lengths_here) - lengths_here
    relative = (dest_here - my_index) % dp_count
    slot_ids = jnp.arange(3, dtype=jnp.int32)

    def pick_entry(values, which):
        return jnp.sum(jnp.where(slot_ids == which, values, 0))

    def slot_of(code):
        return jnp.sum(jnp.where(relative == code, slot_ids, 0))

    chosen = (slot_of(0), slot_of(1), slot_of(dp_count - 1))

    def cut_utterance(source_rows, which):
        start_row = pick_entry(starts, which)
        live_count = pick_entry(lengths_here, which)
        frame_rows = lax.dynamic_slice_in_dim(source_rows, start_row, MAXLEN, 0)
        keep_rows = jnp.arange(MAXLEN, dtype=jnp.int32) < live_count
        kept = jnp.where(keep_rows[:, None], frame_rows, jnp.zeros_like(frame_rows))
        return (kept, jnp.stack([live_count, pick_entry(offsets_here, which)]))

    received, segment = relocate(
        cut_utterance(local_frames, chosen[0]),
        cut_utterance(local_frames, chosen[1]),
        cut_utterance(local_frames, chosen[2]),
    )
    mixed = conv_module(received, segment, params)
    return mixed[None]


def solution(mesh):
    placed = (
        P("group", "dp", None),
        P("group", "dp"),
        P("group", "dp"),
        P("group", "dp"),
        P(("dp", "group")),
        P(("dp", "group"), None),
        P(("dp", "group"), None),
        P(("dp", "group")),
        P(("dp", "group"), None),
    )
    return jax.shard_map(
        shards, mesh=mesh, in_specs=placed, out_specs=P("group", "dp", None), check_vma=False
    )
```

```python
import jax
import jax.numpy as jnp
from jax import lax
from jax.experimental import pallas as pl
from jax.experimental.pallas import tpu as pltpu
from jax.sharding import PartitionSpec as P

D = 2048
KERNEL = 32
MAXLEN = 192
RCV_DEV = 384


epsilon = 1e-05


def shifted(array, axis, by):
    peers = lax.axis_size(axis)
    return lax.ppermute(array, axis, [(i, (i + by) % peers) for i in range(peers)])


def sent_together(arrays, axis, dim, along):
    columns = [a.reshape(*a.shape[:along], -1) for a in arrays]
    both = jnp.concatenate(columns, axis=along)
    out, at, done = (lax.all_gather(both, axis, axis=dim, tiled=True), 0, [])
    for a, column in zip(arrays, columns):
        slab = out[..., at : at + column.shape[along]]
        done.append(slab.reshape(*slab.shape[:along], *a.shape[along:]))
        at += column.shape[along]
    return tuple(done)


def layer_norm(values, scale_gain):
    center = values - jnp.mean(values, axis=-1, keepdims=True)
    spread = jnp.mean(center * center, axis=-1, keepdims=True)
    return center * lax.rsqrt(spread + epsilon) * scale_gain.astype(jnp.float32)


SMALL_WIDTH = 128


def depth_pass(gated_rows, segment, taps, bounds):
    row_count = gated_rows.shape[0]
    margin = KERNEL // 2
    padded = jnp.pad(gated_rows, ((margin, margin), (0, 0)))
    labels = jnp.pad(segment, (margin, margin), constant_values=-1)
    depthwise = jnp.zeros_like(gated_rows)
    for column in range(KERNEL):
        depthwise = depthwise + padded[column : column + row_count] * taps[column : column + 1]
    for bound in bounds:
        start = bound - margin
        window = lax.dynamic_slice_in_dim(padded, start, 2 * KERNEL, 0)
        window_labels = lax.dynamic_slice_in_dim(labels, start, 2 * KERNEL, 0)
        own = lax.dynamic_slice_in_dim(segment, start, KERNEL, 0)
        exact = jnp.zeros((KERNEL, gated_rows.shape[1]), gated_rows.dtype)
        for column in range(KERNEL):
            inside = (window_labels[column : column + KERNEL] == own)[:, None]
            exact = exact + jnp.where(inside, window[column : column + KERNEL], 0.0) * taps[column : column + 1]
        depthwise = lax.dynamic_update_slice_in_dim(depthwise, exact, start, 0)
    return depthwise


def transpose_body(small_ref, out_ref):
    out_ref[...] = jnp.transpose(small_ref[...].astype(jnp.float32))


def small_rows(small_columns):
    count, width = small_columns.shape
    return pl.pallas_call(
        transpose_body,
        out_shape=jax.ShapeDtypeStruct((width, count), jnp.float32),
        in_specs=[pl.BlockSpec(memory_space=pltpu.VMEM)],
        out_specs=pl.BlockSpec(memory_space=pltpu.VMEM),
    )(small_columns)


def conv_module(inputs, segment, bounds, params):
    norm_gain, weight_in, taps, post_gain, weight_out = params
    widths = inputs.shape[1]
    source = inputs.astype(jnp.float32)
    normed = layer_norm(source, norm_gain).astype(jnp.bfloat16)
    projected = jnp.dot(normed, weight_in, preferred_element_type=jnp.float32)
    gated_rows = projected[:, :widths] * jax.nn.sigmoid(projected[:, widths:])
    depthwise = depth_pass(gated_rows, segment, taps, bounds)
    normed_post = layer_norm(depthwise, post_gain)
    active = lax.optimization_barrier((normed_post * jax.nn.sigmoid(normed_post)).astype(jnp.bfloat16))
    return (source + jnp.dot(active, weight_out, preferred_element_type=jnp.float32)).astype(
        jnp.bfloat16
    )


def relocate(own_part, next_part, prev_part):
    from_prev = shifted((next_part[0], next_part[1]), "dp", 1)
    from_next = shifted((prev_part[0], prev_part[1]), "dp", -1)
    received = jnp.zeros((RCV_DEV + MAXLEN, D), jnp.bfloat16)
    segment = jnp.zeros((RCV_DEV,), jnp.int32)
    position = jnp.arange(RCV_DEV, dtype=jnp.int32)
    arrivals = (own_part, from_prev, from_next)
    for label_id in range(3):
        frame_rows, meta_data = arrivals[label_id]
        current = lax.dynamic_slice_in_dim(received, meta_data[1], MAXLEN, 0)
        received = lax.dynamic_update_slice_in_dim(received, current + frame_rows, meta_data[1], 0)
        inside = (position >= meta_data[1]) & (position < meta_data[1] + meta_data[0])
        segment = jnp.where(inside, label_id + 1, segment)
    ordered = jnp.sort(jnp.stack([meta[1] for _, meta in arrivals]))
    return (received[:RCV_DEV], segment, (ordered[1], ordered[2]))


def shards(
    frames, lengths, destination, offsets, norm_gain, weight_in, depth_kernel, post_gain, weight_out
):
    dp_count = lax.axis_size("dp")
    small = jnp.concatenate([norm_gain[:, None], post_gain[:, None], depth_kernel], axis=1)
    small = jnp.pad(small, ((0, 0), (0, SMALL_WIDTH - small.shape[1])))
    both = jnp.concatenate([weight_in, weight_out], axis=1)
    gathered = lax.all_gather(both, ("dp", "group"), axis=0, tiled=True)
    columns = weight_in.shape[1] + weight_out.shape[1]
    peers = lax.axis_size(("dp", "group"))
    copies = jnp.broadcast_to(small[None], (peers,) + small.shape)
    spread = lax.all_to_all(copies, ("dp", "group"), 0, 0, tiled=True)
    small_t = small_rows(spread.reshape(-1, SMALL_WIDTH))
    params = (
        small_t[0:1],
        gathered[:, : weight_in.shape[1]],
        small_t[2 : 2 + KERNEL],
        small_t[1:2],
        gathered[:, weight_in.shape[1] : columns],
    )
    my_index = lax.axis_index("dp")
    local_frames = frames[0]
    lengths_here = lengths[0]
    dest_here = destination[0]
    offsets_here = offsets[0]
    starts = jnp.cumsum(lengths_here) - lengths_here
    relative = (dest_here - my_index) % dp_count
    slot_ids = jnp.arange(3, dtype=jnp.int32)

    def pick_entry(values, which):
        return jnp.sum(jnp.where(slot_ids == which, values, 0))

    def slot_of(code):
        return jnp.sum(jnp.where(relative == code, slot_ids, 0))

    chosen = (slot_of(0), slot_of(1), slot_of(dp_count - 1))

    def cut_utterance(source_rows, which):
        start_row = pick_entry(starts, which)
        live_count = pick_entry(lengths_here, which)
        frame_rows = lax.dynamic_slice_in_dim(source_rows, start_row, MAXLEN, 0)
        keep_rows = jnp.arange(MAXLEN, dtype=jnp.int32) < live_count
        kept = jnp.where(keep_rows[:, None], frame_rows, jnp.zeros_like(frame_rows))
        return (kept, jnp.stack([live_count, pick_entry(offsets_here, which)]))

    received, segment, bounds = relocate(
        cut_utterance(local_frames, chosen[0]),
        cut_utterance(local_frames, chosen[1]),
        cut_utterance(local_frames, chosen[2]),
    )
    mixed = conv_module(received, segment, bounds, params)
    return mixed[None]


def solution(mesh):
    placed = (
        P("group", "dp", None),
        P("group", "dp"),
        P("group", "dp"),
        P("group", "dp"),
        P(("dp", "group")),
        P(("dp", "group"), None),
        P(("dp", "group"), None),
        P(("dp", "group")),
        P(("dp", "group"), None),
    )
    return jax.shard_map(
        shards, mesh=mesh, in_specs=placed, out_specs=P("group", "dp", None), check_vma=False
    )
```

```python
import jax
import jax.numpy as jnp
from jax import lax
from jax.experimental import pallas as pl
from jax.experimental.pallas import tpu as pltpu
from jax.sharding import PartitionSpec as P

D = 2048
KERNEL = 32
MAXLEN = 192
RCV_DEV = 384


epsilon = 1e-05


def shifted(array, axis, by):
    peers = lax.axis_size(axis)
    return lax.ppermute(array, axis, [(i, (i + by) % peers) for i in range(peers)])


def sent_together(arrays, axis, dim, along):
    columns = [a.reshape(*a.shape[:along], -1) for a in arrays]
    both = jnp.concatenate(columns, axis=along)
    out, at, done = (lax.all_gather(both, axis, axis=dim, tiled=True), 0, [])
    for a, column in zip(arrays, columns):
        slab = out[..., at : at + column.shape[along]]
        done.append(slab.reshape(*slab.shape[:along], *a.shape[along:]))
        at += column.shape[along]
    return tuple(done)


def layer_norm(values, scale_gain):
    center = values - jnp.mean(values, axis=-1, keepdims=True)
    spread = jnp.mean(center * center, axis=-1, keepdims=True)
    return center * lax.rsqrt(spread + epsilon) * scale_gain.astype(jnp.float32)


SMALL_WIDTH = 128


def depth_pass(gated_rows, segment, taps, bounds):
    row_count = gated_rows.shape[0]
    margin = KERNEL // 2
    padded = jnp.pad(gated_rows, ((margin, margin), (0, 0)))
    labels = jnp.pad(segment, (margin, margin), constant_values=-1)
    depthwise = jnp.zeros_like(gated_rows)
    for column in range(KERNEL):
        depthwise = depthwise + padded[column : column + row_count] * taps[column : column + 1]
    position = jnp.arange(row_count, dtype=jnp.int32)
    for bound in bounds:
        start = bound - margin
        window, window_labels, own = lax.optimization_barrier(
            (
                lax.dynamic_slice_in_dim(padded, start, 2 * KERNEL, 0),
                lax.dynamic_slice_in_dim(labels, start, 2 * KERNEL, 0),
                lax.dynamic_slice_in_dim(segment, start, KERNEL, 0),
            )
        )
        exact = jnp.zeros((KERNEL, gated_rows.shape[1]), gated_rows.dtype)
        for column in range(KERNEL):
            inside = (window_labels[column : column + KERNEL] == own)[:, None]
            exact = exact + jnp.where(inside, window[column : column + KERNEL], 0.0) * taps[column : column + 1]
        relative = position - start
        placement = (relative[:, None] == jnp.arange(KERNEL, dtype=jnp.int32)[None, :]).astype(jnp.float32)
        placed = jnp.dot(placement, exact, precision=lax.Precision.HIGHEST)
        covered = ((relative >= 0) & (relative < KERNEL))[:, None]
        depthwise = jnp.where(covered, placed, depthwise)
    return depthwise


def transpose_body(small_ref, out_ref):
    out_ref[...] = jnp.transpose(small_ref[...].astype(jnp.float32))


def small_rows(small_columns):
    count, width = small_columns.shape
    return pl.pallas_call(
        transpose_body,
        out_shape=jax.ShapeDtypeStruct((width, count), jnp.float32),
        in_specs=[pl.BlockSpec(memory_space=pltpu.VMEM)],
        out_specs=pl.BlockSpec(memory_space=pltpu.VMEM),
    )(small_columns)


def conv_module(inputs, segment, bounds, params):
    norm_gain, weight_in, taps, post_gain, weight_out = params
    widths = inputs.shape[1]
    source = inputs.astype(jnp.float32)
    normed = layer_norm(source, norm_gain).astype(jnp.bfloat16)
    projected = jnp.dot(normed, weight_in, preferred_element_type=jnp.float32)
    gated_rows = projected[:, :widths] * jax.nn.sigmoid(projected[:, widths:])
    depthwise = depth_pass(gated_rows, segment, taps, bounds)
    normed_post = layer_norm(depthwise, post_gain)
    active = (normed_post * jax.nn.sigmoid(normed_post)).astype(jnp.bfloat16)
    return (source + jnp.dot(active, weight_out, preferred_element_type=jnp.float32)).astype(
        jnp.bfloat16
    )


def relocate(own_part, next_part, prev_part):
    from_prev = shifted((next_part[0], next_part[1]), "dp", 1)
    from_next = shifted((prev_part[0], prev_part[1]), "dp", -1)
    received = jnp.zeros((RCV_DEV + MAXLEN, D), jnp.bfloat16)
    segment = jnp.zeros((RCV_DEV,), jnp.int32)
    position = jnp.arange(RCV_DEV, dtype=jnp.int32)
    arrivals = (own_part, from_prev, from_next)
    for label_id in range(3):
        frame_rows, meta_data = arrivals[label_id]
        current = lax.dynamic_slice_in_dim(received, meta_data[1], MAXLEN, 0)
        received = lax.dynamic_update_slice_in_dim(received, current + frame_rows, meta_data[1], 0)
        inside = (position >= meta_data[1]) & (position < meta_data[1] + meta_data[0])
        segment = jnp.where(inside, label_id + 1, segment)
    ordered = jnp.sort(jnp.stack([meta[1] for _, meta in arrivals]))
    return (received[:RCV_DEV], segment, (ordered[1], ordered[2]))


def shards(
    frames, lengths, destination, offsets, norm_gain, weight_in, depth_kernel, post_gain, weight_out
):
    dp_count = lax.axis_size("dp")
    small = jnp.concatenate([norm_gain[:, None], post_gain[:, None], depth_kernel], axis=1)
    small = jnp.pad(small, ((0, 0), (0, SMALL_WIDTH - small.shape[1])))
    both = jnp.concatenate([weight_in, weight_out], axis=1)
    gathered = lax.all_gather(both, ("dp", "group"), axis=0, tiled=True)
    columns = weight_in.shape[1] + weight_out.shape[1]
    peers = lax.axis_size(("dp", "group"))
    copies = jnp.broadcast_to(small[None], (peers,) + small.shape)
    spread = lax.all_to_all(copies, ("dp", "group"), 0, 0, tiled=True)
    small_t = small_rows(spread.reshape(-1, SMALL_WIDTH))
    params = (
        small_t[0:1],
        gathered[:, : weight_in.shape[1]],
        small_t[2 : 2 + KERNEL],
        small_t[1:2],
        gathered[:, weight_in.shape[1] : columns],
    )
    my_index = lax.axis_index("dp")
    local_frames = frames[0]
    lengths_here = lengths[0]
    dest_here = destination[0]
    offsets_here = offsets[0]
    starts = jnp.cumsum(lengths_here) - lengths_here
    relative = (dest_here - my_index) % dp_count
    slot_ids = jnp.arange(3, dtype=jnp.int32)

    def pick_entry(values, which):
        return jnp.sum(jnp.where(slot_ids == which, values, 0))

    def slot_of(code):
        return jnp.sum(jnp.where(relative == code, slot_ids, 0))

    chosen = (slot_of(0), slot_of(1), slot_of(dp_count - 1))

    def cut_utterance(source_rows, which):
        start_row = pick_entry(starts, which)
        live_count = pick_entry(lengths_here, which)
        frame_rows = lax.dynamic_slice_in_dim(source_rows, start_row, MAXLEN, 0)
        keep_rows = jnp.arange(MAXLEN, dtype=jnp.int32) < live_count
        kept = jnp.where(keep_rows[:, None], frame_rows, jnp.zeros_like(frame_rows))
        return (kept, jnp.stack([live_count, pick_entry(offsets_here, which)]))

    received, segment, bounds = relocate(
        cut_utterance(local_frames, chosen[0]),
        cut_utterance(local_frames, chosen[1]),
        cut_utterance(local_frames, chosen[2]),
    )
    mixed = conv_module(received, segment, bounds, params)
    return mixed[None]


def solution(mesh):
    placed = (
        P("group", "dp", None),
        P("group", "dp"),
        P("group", "dp"),
        P("group", "dp"),
        P(("dp", "group")),
        P(("dp", "group"), None),
        P(("dp", "group"), None),
        P(("dp", "group")),
        P(("dp", "group"), None),
    )
    return jax.shard_map(
        shards, mesh=mesh, in_specs=placed, out_specs=P("group", "dp", None), check_vma=False
    )
```

```python
import jax
import jax.numpy as jnp
from jax import lax
from jax.experimental import pallas as pl
from jax.experimental.pallas import tpu as pltpu
from jax.sharding import PartitionSpec as P

D = 2048
KERNEL = 32
MAXLEN = 192
RCV_DEV = 384


epsilon = 1e-05


def shifted(array, axis, by):
    peers = lax.axis_size(axis)
    return lax.ppermute(array, axis, [(i, (i + by) % peers) for i in range(peers)])


def sent_together(arrays, axis, dim, along):
    columns = [a.reshape(*a.shape[:along], -1) for a in arrays]
    both = jnp.concatenate(columns, axis=along)
    out, at, done = (lax.all_gather(both, axis, axis=dim, tiled=True), 0, [])
    for a, column in zip(arrays, columns):
        slab = out[..., at : at + column.shape[along]]
        done.append(slab.reshape(*slab.shape[:along], *a.shape[along:]))
        at += column.shape[along]
    return tuple(done)


def layer_norm(values, scale_gain):
    center = values - jnp.mean(values, axis=-1, keepdims=True)
    spread = jnp.mean(center * center, axis=-1, keepdims=True)
    return center * lax.rsqrt(spread + epsilon) * scale_gain.astype(jnp.float32)


SMALL_WIDTH = 128


def depth_pass(gated_rows, segment, taps):
    row_count = gated_rows.shape[0]
    margin = KERNEL // 2
    padded = jnp.pad(gated_rows, ((margin, margin), (0, 0)))
    labels = jnp.pad(segment, (margin, margin), constant_values=-1)
    depthwise = jnp.zeros_like(gated_rows)
    for column in range(KERNEL):
        inside = (labels[column : column + row_count] == segment)[:, None]
        depthwise = depthwise + jnp.where(inside, padded[column : column + row_count], 0.0) * taps[column : column + 1]
    return depthwise


def transpose_body(small_ref, out_ref):
    out_ref[...] = jnp.transpose(small_ref[...].astype(jnp.float32))


def small_rows(small_columns):
    count, width = small_columns.shape
    return pl.pallas_call(
        transpose_body,
        out_shape=jax.ShapeDtypeStruct((width, count), jnp.float32),
        in_specs=[pl.BlockSpec(memory_space=pltpu.VMEM)],
        out_specs=pl.BlockSpec(memory_space=pltpu.VMEM),
    )(small_columns)


def conv_module(inputs, segment, params):
    norm_gain, weight_in, taps, post_gain, weight_out = params
    widths = inputs.shape[1]
    source = inputs.astype(jnp.float32)
    normed = layer_norm(source, norm_gain).astype(jnp.bfloat16)
    projected = jnp.dot(normed, weight_in, preferred_element_type=jnp.float32)
    gated_rows = projected[:, :widths] * jax.nn.sigmoid(projected[:, widths:])
    depthwise = depth_pass(gated_rows, segment, taps)
    normed_post = layer_norm(depthwise, post_gain)
    active = (normed_post * jax.nn.sigmoid(normed_post)).astype(jnp.bfloat16)
    return (source + jnp.dot(active, weight_out, preferred_element_type=jnp.float32)).astype(
        jnp.bfloat16
    )


def relocate(own_part, next_part, prev_part):
    from_prev = shifted((next_part[0], next_part[1]), "dp", 1)
    from_next = shifted((prev_part[0], prev_part[1]), "dp", -1)
    received = jnp.zeros((RCV_DEV + MAXLEN, D), jnp.bfloat16)
    segment = jnp.zeros((RCV_DEV,), jnp.int32)
    position = jnp.arange(RCV_DEV, dtype=jnp.int32)
    arrivals = (own_part, from_prev, from_next)
    for label_id in range(3):
        frame_rows, meta_data = arrivals[label_id]
        current = lax.dynamic_slice_in_dim(received, meta_data[1], MAXLEN, 0)
        received = lax.dynamic_update_slice_in_dim(received, current + frame_rows, meta_data[1], 0)
        inside = (position >= meta_data[1]) & (position < meta_data[1] + meta_data[0])
        segment = jnp.where(inside, label_id + 1, segment)
    return (received[:RCV_DEV], segment)


def shards(
    frames, lengths, destination, offsets, norm_gain, weight_in, depth_kernel, post_gain, weight_out
):
    dp_count = lax.axis_size("dp")
    small = jnp.concatenate([norm_gain[:, None], post_gain[:, None], depth_kernel], axis=1)
    small = jnp.pad(small, ((0, 0), (0, SMALL_WIDTH - small.shape[1])))
    both = jnp.concatenate([weight_in, weight_out], axis=1)
    gathered = lax.all_gather(
        lax.all_gather(both, "group", axis=0, tiled=True), "dp", axis=0, tiled=True
    )
    columns = weight_in.shape[1] + weight_out.shape[1]
    peers = lax.axis_size(("dp", "group"))
    copies = jnp.broadcast_to(small[None], (peers,) + small.shape)
    spread = lax.all_to_all(copies, ("dp", "group"), 0, 0, tiled=True)
    small_t = small_rows(spread.reshape(-1, SMALL_WIDTH))
    params = (
        small_t[0:1],
        gathered[:, : weight_in.shape[1]],
        small_t[2 : 2 + KERNEL],
        small_t[1:2],
        gathered[:, weight_in.shape[1] : columns],
    )
    my_index = lax.axis_index("dp")
    local_frames = frames[0]
    lengths_here = lengths[0]
    dest_here = destination[0]
    offsets_here = offsets[0]
    starts = jnp.cumsum(lengths_here) - lengths_here
    relative = (dest_here - my_index) % dp_count
    slot_ids = jnp.arange(3, dtype=jnp.int32)

    def pick_entry(values, which):
        return jnp.sum(jnp.where(slot_ids == which, values, 0))

    def slot_of(code):
        return jnp.sum(jnp.where(relative == code, slot_ids, 0))

    chosen = (slot_of(0), slot_of(1), slot_of(dp_count - 1))

    def cut_utterance(source_rows, which):
        start_row = pick_entry(starts, which)
        live_count = pick_entry(lengths_here, which)
        frame_rows = lax.dynamic_slice_in_dim(source_rows, start_row, MAXLEN, 0)
        keep_rows = jnp.arange(MAXLEN, dtype=jnp.int32) < live_count
        kept = jnp.where(keep_rows[:, None], frame_rows, jnp.zeros_like(frame_rows))
        return (kept, jnp.stack([live_count, pick_entry(offsets_here, which)]))

    received, segment = relocate(
        cut_utterance(local_frames, chosen[0]),
        cut_utterance(local_frames, chosen[1]),
        cut_utterance(local_frames, chosen[2]),
    )
    mixed = conv_module(received, segment, params)
    return mixed[None]


def solution(mesh):
    placed = (
        P("group", "dp", None),
        P("group", "dp"),
        P("group", "dp"),
        P("group", "dp"),
        P(("dp", "group")),
        P(("dp", "group"), None),
        P(("dp", "group"), None),
        P(("dp", "group")),
        P(("dp", "group"), None),
    )
    return jax.shard_map(
        shards, mesh=mesh, in_specs=placed, out_specs=P("group", "dp", None), check_vma=False
    )
```

```python
import functools

import jax
import jax.numpy as jnp
from jax import lax
from jax.experimental import pallas as pl
from jax.experimental.pallas import tpu as pltpu
from jax.sharding import PartitionSpec as P

D = 2048
KERNEL = 32
MAXLEN = 192
RCV_DEV = 384


epsilon = 1e-05


def shifted(array, axis, by):
    peers = lax.axis_size(axis)
    return lax.ppermute(array, axis, [(i, (i + by) % peers) for i in range(peers)])


def sent_together(arrays, axis, dim, along):
    columns = [a.reshape(*a.shape[:along], -1) for a in arrays]
    both = jnp.concatenate(columns, axis=along)
    out, at, done = (lax.all_gather(both, axis, axis=dim, tiled=True), 0, [])
    for a, column in zip(arrays, columns):
        slab = out[..., at : at + column.shape[along]]
        done.append(slab.reshape(*slab.shape[:along], *a.shape[along:]))
        at += column.shape[along]
    return tuple(done)


def layer_norm(values, scale_gain):
    center = values - jnp.mean(values, axis=-1, keepdims=True)
    spread = jnp.mean(center * center, axis=-1, keepdims=True)
    return center * lax.rsqrt(spread + epsilon) * scale_gain.astype(jnp.float32)


SMALL_WIDTH = 128


def depth_pass(gated_rows, taps):
    row_count = gated_rows.shape[0]
    margin = KERNEL // 2
    padded = jnp.pad(gated_rows, ((margin, margin), (0, 0)))
    depthwise = jnp.zeros_like(gated_rows)
    for column in range(KERNEL):
        depthwise = depthwise + padded[column : column + row_count] * taps[column : column + 1]
    return depthwise


def group_gather_body(groups, first_ref, second_ref, out_ref, send_sems, recv_sems):
    me = lax.axis_index("group")
    here = lax.axis_index("dp")
    rows, split = first_ref.shape
    parts = ((first_ref, 0, split), (second_ref, split, second_ref.shape[1]))
    mesh_ids = pl.DeviceIdType.MESH

    def target(owner, low, width):
        return out_ref.at[pl.ds(pl.multiple_of(owner * rows, rows), rows), pl.ds(low, width)]

    for source_ref, low, width in parts:
        out_ref[pl.ds(pl.multiple_of(me * rows, rows), rows), pl.ds(low, width)] = source_ref[...]
    barrier = pltpu.get_barrier_semaphore()
    for step in range(1, groups):
        peer = lax.rem(me + step, groups)
        pl.semaphore_signal(barrier, inc=1, device_id=(here, peer), device_id_type=mesh_ids)
    pl.semaphore_wait(barrier, groups - 1)
    sends = []
    for step in range(1, groups):
        peer = lax.rem(me + step, groups)
        for index, (source_ref, low, width) in enumerate(parts):
            slot = 2 * (step - 1) + index
            copy = pltpu.make_async_remote_copy(
                src_ref=source_ref,
                dst_ref=target(me, low, width),
                send_sem=send_sems.at[slot],
                recv_sem=recv_sems.at[slot],
                device_id=(here, peer),
                device_id_type=mesh_ids,
            )
            copy.start()
            sends.append(copy)
    for copy in sends:
        copy.wait_send()
    for step in range(1, groups):
        source = lax.rem(me + groups - step, groups)
        for index, (source_ref, low, width) in enumerate(parts):
            slot = 2 * (step - 1) + index
            incoming = pltpu.make_async_remote_copy(
                src_ref=source_ref,
                dst_ref=target(source, low, width),
                send_sem=send_sems.at[slot],
                recv_sem=recv_sems.at[slot],
                device_id=(here, source),
                device_id_type=mesh_ids,
            )
            incoming.wait_recv()


def group_gather(first, second):
    groups = lax.axis_size("group")
    rows = first.shape[0]
    width = first.shape[1] + second.shape[1]
    return pl.pallas_call(
        functools.partial(group_gather_body, groups),
        out_shape=jax.ShapeDtypeStruct((groups * rows, width), first.dtype),
        in_specs=[pl.BlockSpec(memory_space=pltpu.VMEM)] * 2,
        out_specs=pl.BlockSpec(memory_space=pltpu.VMEM),
        scratch_shapes=[
            pltpu.SemaphoreType.DMA((2 * (groups - 1),)),
            pltpu.SemaphoreType.DMA((2 * (groups - 1),)),
        ],
        compiler_params=pltpu.CompilerParams(collective_id=0, has_side_effects=True),
    )(first, second)


def transpose_body(small_ref, out_ref):
    out_ref[...] = jnp.transpose(small_ref[...].astype(jnp.float32))


def small_rows(small_columns):
    count, width = small_columns.shape
    return pl.pallas_call(
        transpose_body,
        out_shape=jax.ShapeDtypeStruct((width, count), jnp.float32),
        in_specs=[pl.BlockSpec(memory_space=pltpu.VMEM)],
        out_specs=pl.BlockSpec(memory_space=pltpu.VMEM),
    )(small_columns)


def conv_module(inputs, bounds, params):
    norm_gain, weight_in, taps, post_gain, weight_out = params
    widths = inputs.shape[1]
    source = inputs.astype(jnp.float32)
    normed = lax.optimization_barrier(layer_norm(source, norm_gain).astype(jnp.bfloat16))
    values = jnp.dot(normed, weight_in[:, :widths], preferred_element_type=jnp.float32)
    gates = jnp.dot(normed, weight_in[:, widths:], preferred_element_type=jnp.float32)
    gated_rows = values * jax.nn.sigmoid(gates)
    depthwise = depth_pass(gated_rows, taps)
    normed_post = layer_norm(depthwise, post_gain)
    active = (normed_post * jax.nn.sigmoid(normed_post)).astype(jnp.bfloat16)
    spaced = (source + jnp.dot(active, weight_out, preferred_element_type=jnp.float32)).astype(
        jnp.bfloat16
    )
    gap = KERNEL // 2
    position = jnp.arange(RCV_DEV, dtype=jnp.int32)[:, None]
    return jnp.where(
        position < bounds[0],
        spaced[:RCV_DEV],
        jnp.where(position < bounds[1], spaced[gap : gap + RCV_DEV], spaced[2 * gap : 2 * gap + RCV_DEV]),
    )


def relocate(own_part, next_part, prev_part):
    from_prev = shifted((next_part[0], next_part[1]), "dp", 1)
    from_next = shifted((prev_part[0], prev_part[1]), "dp", -1)
    arrivals = (own_part, from_prev, from_next)
    gap = KERNEL // 2
    starts = [meta[1] for _, meta in arrivals]
    received = jnp.zeros((RCV_DEV + 4 * gap + MAXLEN, D), jnp.bfloat16)
    for index, (frame_rows, meta_data) in enumerate(arrivals):
        rank = sum((starts[other] < starts[index]).astype(jnp.int32) for other in range(3) if other != index)
        at = starts[index] + gap * (rank + 1)
        current = lax.dynamic_slice_in_dim(received, at, MAXLEN, 0)
        received = lax.dynamic_update_slice_in_dim(received, current + frame_rows, at, 0)
    ordered = jnp.sort(jnp.stack(starts))
    return (received[gap : gap + RCV_DEV + 2 * gap], (ordered[1], ordered[2]))


def shards(
    frames, lengths, destination, offsets, norm_gain, weight_in, depth_kernel, post_gain, weight_out
):
    dp_count = lax.axis_size("dp")
    small = jnp.concatenate([norm_gain[:, None], post_gain[:, None], depth_kernel], axis=1)
    small = jnp.pad(small, ((0, 0), (0, SMALL_WIDTH - small.shape[1])))
    gathered = lax.all_gather(
        group_gather(weight_in, weight_out), "dp", axis=0, tiled=True
    )
    columns = weight_in.shape[1] + weight_out.shape[1]
    peers = lax.axis_size(("dp", "group"))
    copies = jnp.broadcast_to(small[None], (peers,) + small.shape)
    spread = lax.all_to_all(copies, ("dp", "group"), 0, 0, tiled=True)
    small_t = small_rows(spread.reshape(-1, SMALL_WIDTH))
    params = (
        small_t[0:1],
        gathered[:, : weight_in.shape[1]],
        small_t[2 : 2 + KERNEL],
        small_t[1:2],
        gathered[:, weight_in.shape[1] : columns],
    )
    my_index = lax.axis_index("dp")
    local_frames = frames[0]
    lengths_here = lengths[0]
    dest_here = destination[0]
    offsets_here = offsets[0]
    starts = jnp.cumsum(lengths_here) - lengths_here
    relative = (dest_here - my_index) % dp_count
    slot_ids = jnp.arange(3, dtype=jnp.int32)

    def pick_entry(values, which):
        return jnp.sum(jnp.where(slot_ids == which, values, 0))

    def slot_of(code):
        return jnp.sum(jnp.where(relative == code, slot_ids, 0))

    chosen = (slot_of(0), slot_of(1), slot_of(dp_count - 1))

    def cut_utterance(source_rows, which):
        start_row = pick_entry(starts, which)
        live_count = pick_entry(lengths_here, which)
        frame_rows = lax.dynamic_slice_in_dim(source_rows, start_row, MAXLEN, 0)
        keep_rows = jnp.arange(MAXLEN, dtype=jnp.int32) < live_count
        kept = jnp.where(keep_rows[:, None], frame_rows, jnp.zeros_like(frame_rows))
        return (kept, jnp.stack([live_count, pick_entry(offsets_here, which)]))

    received, bounds = relocate(
        cut_utterance(local_frames, chosen[0]),
        cut_utterance(local_frames, chosen[1]),
        cut_utterance(local_frames, chosen[2]),
    )
    mixed = conv_module(received, bounds, params)
    return mixed[None]


def solution(mesh):
    placed = (
        P("group", "dp", None),
        P("group", "dp"),
        P("group", "dp"),
        P("group", "dp"),
        P(("dp", "group")),
        P(("dp", "group"), None),
        P(("dp", "group"), None),
        P(("dp", "group")),
        P(("dp", "group"), None),
    )
    return jax.shard_map(
        shards, mesh=mesh, in_specs=placed, out_specs=P("group", "dp", None), check_vma=False
    )
```
